768 devices in a mesh: grp: 192 (over z, y_hi, x, core), gy: 4 (over y_lo).
Axes of the slice: x: 4, y: 8 (y_hi: 2, y_lo: 4; y = y_hi * 4 + y_lo), z: 12, core: 2. Of those that a mesh axis runs over, the one named last changes fastest.
Arguments:
- potential_warmth: float32 [24, 3072, 2048], P(None, 'grp', 'gy'), may hold values from -2 to 4
- saltiness_anomaly: float32 [24, 3072, 2048], P(None, 'grp', 'gy'), may hold values from -6 to 6
- seawater_velocity: float32 [2, 3072, 2048], P(None, 'grp', 'gy'), may hold values from -2 to 2
- airflow_surface_forcing: float32 [2, 3072, 2048], P(None, 'grp', 'gy'), may hold values from -3 to 3
- glacial_velocity_sigma: float32 [5, 3072, 2048], P(None, 'grp', 'gy'), may hold values from -3 to 3
- category_coverage: float32 [5, 3072, 2048], P(None, 'grp', 'gy'), may hold values from 0.17 to 0.2
- category_thickness: float32 [5, 3072, 2048], P(None, 'grp', 'gy'), may hold values from 0.2 to 1
- seawater_indicator: int32 [3072, 2048], P('grp', 'gy'), may hold values from 0 to 1
- dynamics_indicator: int32 [3072, 2048], P('grp', 'gy'), may hold values from 0 to 1, as said below
- patch_home_position: int32 [192, 16], P('grp', 'gy'), may hold values from -1 to 3, as said below
Outputs:
- potential_warmth_updated: float32 [24, 3072, 2048], P(None, 'grp', 'gy')
- saltiness_updated: float32 [24, 3072, 2048], P(None, 'grp', 'gy')
- coupled_surface_velocity: float32 [2, 3072, 2048], P(None, 'grp', 'gy')
- glacial_patch_update: float32 [5, 3072, 2048], P(None, 'grp', 'gy')
The draws below stay inside these ranges and needn't reach their ends.
Inputs may be any that keep to these rules, and one draw needn't show every extreme that they name: For a block with ice, patch_home_position = d + p: it goes to slot p from its tile of the device with the same grp index and gy index d; no two blocks of one tile share a value; the first tile row holds 4 blocks with ice in every draw. `dynamics_indicator`: 1 only at cells with seawater_indicator 1 inside blocks whose patch_home_position is not negative.
All inputs are finite; a program needn't handle non-finite values.
Results may differ from the reference program's by a relative error of at most 0.0003.
Values sent between devices are 32-bit elements; how exact they have to be, the bound alone decides.
No kernel may reach another device: no remote copies, remote signals or barrier semaphores. Data moves between devices by JAX's collectives and lax.ppermute only.
A program may use at most 32 MiB of HBM per device.

```python
import math
import jax
import jax.numpy as jnp
from jax import lax

CX = 16
BY = 128
NB = 4
NSUB = 4
VERTICAL_COUNT = 24
NCAT = 5
PAIR = 1
GRID_EAST_COUNT = 3072
GRID_NORTH_COUNT = 2048
NBY = 16
N_GRP = 192
N_GY = 4


def routing_tables(key):
    cell_key = jax.random.fold_in(key, 11)
    block_key = jax.random.fold_in(key, 12)
    rotate_key = jax.random.fold_in(key, 13)
    speck_key = jax.random.fold_in(key, 14)
    seawater_points = (jax.random.randint(cell_key, (GRID_EAST_COUNT, GRID_NORTH_COUNT), 0, 8) != 0).astype(jnp.int32)
    block_row = jnp.arange(NBY, dtype=jnp.int32)
    polar_rows = (block_row < NB) | (block_row >= NBY - NB // 2)
    random_ice = jax.random.randint(block_key, (N_GRP, NBY), 0, 3) == 0
    iced_blocks = (polar_rows[None, :] | random_ice).astype(jnp.int32)
    tile_blocks = iced_blocks.reshape(N_GRP, N_GY, NB)
    order_rank = jnp.cumsum(tile_blocks, axis=2) - tile_blocks
    rotation = jax.random.randint(rotate_key, (N_GRP, N_GY, 1), 0, N_GY)
    slot_value = (rotation + order_rank) % N_GY * PAIR + order_rank // N_GY
    patch_home_position = jnp.where(tile_blocks > 0, slot_value, -1).reshape(N_GRP, NBY).astype(jnp.int32)
    cell_iced = jnp.repeat(jnp.repeat(iced_blocks, CX, axis=0), BY, axis=1)
    speckles = (jax.random.randint(speck_key, (GRID_EAST_COUNT, GRID_NORTH_COUNT), 0, 4) != 0).astype(jnp.int32)
    ice_cells = seawater_points * cell_iced * speckles
    return (seawater_points, ice_cells, patch_home_position)


def draw_seawater_indicator(key, part):
    return routing_tables(key)[0]


def draw_dynamics_indicator(key, part):
    return routing_tables(key)[1]


def draw_patch_home_position(key, part):
    return routing_tables(key)[2]


def block_scale(rng, shape, shards, least, high):
    gain = 1.0
    for position, shards_of in shards:
        steps = jax.random.uniform(jax.random.fold_in(jax.random.fold_in(rng, 6), position), (shards_of,), jnp.float32, least / len(shards), high / len(shards))
        gain = gain * jnp.repeat(jnp.exp(steps), shape[position] // shards_of).reshape((-1,) + (1,) * (len(shape) - 1 - position))
    return gain


def normal_values(own_key, shape, scale, bound, pieces=(), kind=jnp.bfloat16):
    array = scale * jax.random.normal(own_key, shape, jnp.float32)
    if pieces:
        array = array * block_scale(own_key, shape, pieces, -0.22, 0.18)
    return jnp.clip(array, -bound, bound).astype(kind)


def setup_inputs(seed: int = 0) -> dict:
    key_of = jax.random.split(jax.random.key(seed), 11)
    potential_warmth = jnp.clip(-2.0 + 6.0 * jax.random.uniform(key_of[0], (VERTICAL_COUNT, GRID_EAST_COUNT, GRID_NORTH_COUNT), jnp.float32) ** block_scale(key_of[0], (VERTICAL_COUNT, GRID_EAST_COUNT, GRID_NORTH_COUNT), ((1, 192), (2, 4)), -0.2, 0.2), -2.0, 4.0)
    saltiness_anomaly = normal_values(key_of[1], (VERTICAL_COUNT, GRID_EAST_COUNT, GRID_NORTH_COUNT), 1.0, 6.0, ((1, 192), (2, 4)), jnp.float32)
    seawater_velocity = normal_values(key_of[2], (2, GRID_EAST_COUNT, GRID_NORTH_COUNT), 0.3, 2.0, ((1, 192), (2, 4)), jnp.float32)
    airflow_surface_forcing = normal_values(key_of[3], (2, GRID_EAST_COUNT, GRID_NORTH_COUNT), 0.5, 3.0, ((1, 192), (2, 4)), jnp.float32)
    glacial_velocity_sigma = normal_values(key_of[4], (5, GRID_EAST_COUNT, GRID_NORTH_COUNT), 0.5, 3.0, ((1, 192), (2, 4)), jnp.float32)
    category_coverage = jnp.clip(0.17 + 0.030000001 * jax.random.uniform(key_of[5], (NCAT, GRID_EAST_COUNT, GRID_NORTH_COUNT), jnp.float32) ** block_scale(key_of[5], (NCAT, GRID_EAST_COUNT, GRID_NORTH_COUNT), ((1, 192), (2, 4)), -0.2, 0.2), 0.17, 0.2)
    category_thickness = jnp.clip(jnp.exp(math.log(1.0) - 1.609438 * jax.random.uniform(key_of[6], (NCAT, GRID_EAST_COUNT, GRID_NORTH_COUNT), jnp.float32) ** block_scale(key_of[6], (NCAT, GRID_EAST_COUNT, GRID_NORTH_COUNT), ((1, 192), (2, 4)), -0.2, 0.2)), 0.2, 1.0)
    seawater_indicator = draw_seawater_indicator(jax.random.fold_in(key_of[10], 71), 0)
    dynamics_indicator = draw_dynamics_indicator(jax.random.fold_in(key_of[10], 71), 0)
    patch_home_position = draw_patch_home_position(jax.random.fold_in(key_of[10], 71), 0)
    return dict(potential_warmth=potential_warmth, saltiness_anomaly=saltiness_anomaly, seawater_velocity=seawater_velocity, airflow_surface_forcing=airflow_surface_forcing, glacial_velocity_sigma=glacial_velocity_sigma, category_coverage=category_coverage, category_thickness=category_thickness, seawater_indicator=seawater_indicator, dynamics_indicator=dynamics_indicator, patch_home_position=patch_home_position)


DIFFUSIVITY = 0.2
STRENGTH_COEF = 20.0
MIN_MASS = 0.5
RELAX_RATE = 0.5
ECCENTRIC = 4.0
DELTA_FLOOR = 0.0025
SPEED_FLOOR = 0.01
CORIOLIS = 0.5
HEAT_COEF = 4.0
THIN_LIMIT = 0.1
FREEZING = -1.8
WARMTH_FACTOR = 0.05
STRESS_SCALE = 0.5

def east_of(field, offset):
    return jnp.roll(field, -offset, axis=-2)

def north_of(field, offset):
    border = jnp.zeros_like(field[..., :1])
    if offset > 0:
        return jnp.concatenate([field[..., 1:], border], axis=-1)
    return jnp.concatenate([border, field[..., :-1]], axis=-1)

def evp_subcycles(vel_u, vel_v, sig_one, sig_two, sig_shear, cur_u, cur_v, concentration, thickness, wind_u, wind_v, glacial_indicator):
    strength = thickness * jnp.exp(-STRENGTH_COEF * (1.0 - concentration))
    ice_mass = thickness + MIN_MASS
    for subcycle in range(NSUB):
        u_east = east_of(vel_u, 1) - vel_u
        v_north = north_of(vel_v, 1) - vel_v
        u_north = north_of(vel_u, 1) - vel_u
        v_east = east_of(vel_v, 1) - vel_v
        divergence = u_east + v_north
        tension = u_east - v_north
        shear_rate = u_north + v_east
        deform_rate = jnp.sqrt(divergence * divergence + (tension * tension + shear_rate * shear_rate) / ECCENTRIC + DELTA_FLOOR)
        viscous = strength / deform_rate
        sig_one = glacial_indicator * (sig_one + RELAX_RATE * (viscous * divergence - strength)) / (1.0 + RELAX_RATE)
        sig_two = glacial_indicator * (sig_two + RELAX_RATE * viscous * tension / ECCENTRIC) / (1.0 + RELAX_RATE)
        sig_shear = glacial_indicator * (sig_shear + RELAX_RATE * viscous * shear_rate / ECCENTRIC) / (1.0 + RELAX_RATE)
        back_one_x = sig_one - east_of(sig_one, -1)
        back_two_x = sig_two - east_of(sig_two, -1)
        back_one_y = sig_one - north_of(sig_one, -1)
        back_two_y = sig_two - north_of(sig_two, -1)
        force_u = 0.5 * (back_one_x + back_two_x) + (sig_shear - north_of(sig_shear, -1))
        force_v = 0.5 * (back_one_y - back_two_y) + (sig_shear - east_of(sig_shear, -1))
        rel_speed = jnp.sqrt((cur_u - vel_u) ** 2 + (cur_v - vel_v) ** 2 + SPEED_FLOOR)
        water_coef = concentration * rel_speed
        implicit = ice_mass + water_coef
        new_u = glacial_indicator * (ice_mass * vel_u + force_u + wind_u + water_coef * cur_u + CORIOLIS * ice_mass * vel_v) / implicit
        new_v = glacial_indicator * (ice_mass * vel_v + force_v + wind_v + water_coef * cur_v - CORIOLIS * ice_mass * vel_u) / implicit
        vel_u, vel_v = (new_u, new_v)
    rel_speed = jnp.sqrt((cur_u - vel_u) ** 2 + (cur_v - vel_v) ** 2 + SPEED_FLOOR)
    water_coef = concentration * rel_speed
    stress_u = glacial_indicator * water_coef * (vel_u - cur_u)
    stress_v = glacial_indicator * water_coef * (vel_v - cur_v)
    return ((vel_u, vel_v, sig_one, sig_two, sig_shear), (stress_u, stress_v))

def seabed_exchange(surface_temp, category_coverage, category_thickness, glacial_indicator, cat_axis):
    per_cat = HEAT_COEF * category_coverage * category_coverage / (category_thickness + THIN_LIMIT * category_coverage)
    return glacial_indicator * (surface_temp - FREEZING) * lax.optimization_barrier(jnp.sum(per_cat, axis=cat_axis))

def reference(potential_warmth, saltiness_anomaly, seawater_velocity, airflow_surface_forcing, glacial_velocity_sigma, category_coverage, category_thickness, seawater_indicator, dynamics_indicator, patch_home_position):
    seawater_points = seawater_indicator.astype(jnp.float32)
    glacial_indicator = dynamics_indicator.astype(jnp.float32)
    concentration = lax.optimization_barrier(jnp.sum(category_coverage, axis=0))
    thickness = lax.optimization_barrier(jnp.sum(category_thickness, axis=0))

    def diffuse_quantity(field):
        inflow = jnp.zeros_like(field)
        for near_field, near_wet in ((east_of(field, 1), east_of(seawater_points, 1)), (east_of(field, -1), east_of(seawater_points, -1)), (north_of(field, 1), north_of(seawater_points, 1)), (north_of(field, -1), north_of(seawater_points, -1))):
            inflow = inflow + near_wet * (near_field - field)
        return field + DIFFUSIVITY * seawater_points * inflow
    state, stress = evp_subcycles(glacial_velocity_sigma[0], glacial_velocity_sigma[1], glacial_velocity_sigma[2], glacial_velocity_sigma[3], glacial_velocity_sigma[4], seawater_velocity[0], seawater_velocity[1], concentration, thickness, airflow_surface_forcing[0], airflow_surface_forcing[1], glacial_indicator)
    heat_exchange = seabed_exchange(potential_warmth[0], category_coverage, category_thickness, glacial_indicator, 0)
    potential_warmth_updated = diffuse_quantity(potential_warmth)
    potential_warmth_updated = potential_warmth_updated.at[0].add(-WARMTH_FACTOR * seawater_points * heat_exchange)
    saltiness_updated = diffuse_quantity(saltiness_anomaly)
    coupled_surface_velocity = seawater_points * (seawater_velocity + STRESS_SCALE * jnp.stack(stress))
    ice_new = jnp.stack(state)
    blocks = ice_new.reshape(5, N_GRP, CX, NBY, BY).transpose(1, 3, 0, 2, 4)
    tile_row = (jnp.arange(NBY, dtype=jnp.int32) // NB).astype(jnp.int32)
    target = jnp.where(patch_home_position >= 0, patch_home_position // PAIR * NB + tile_row[None, :] * PAIR + patch_home_position % PAIR, NBY).astype(jnp.int32)
    grp_rows = jnp.arange(N_GRP, dtype=jnp.int32)[:, None]
    placed = jnp.zeros((N_GRP, NBY + 1, 5, CX, BY), jnp.float32)
    placed = placed.at[grp_rows, target].set(blocks)
    glacial_patch_update = placed[:, :NBY].transpose(2, 0, 3, 1, 4).reshape(5, GRID_EAST_COUNT, GRID_NORTH_COUNT)
    return (potential_warmth_updated, saltiness_updated, coupled_surface_velocity, glacial_patch_update)
```

```python
import jax
import jax.numpy as jnp
from jax import lax
from jax.experimental import pallas as pl
from jax.experimental.pallas import tpu as pltpu
from jax.sharding import PartitionSpec as P


NSUB = 4
DIFFUSIVITY = 0.2
STRENGTH_COEF = 20.0
MIN_MASS = 0.5
RELAX_RATE = 0.5
ECCENTRIC = 4.0
DELTA_FLOOR = 0.0025
SPEED_FLOOR = 0.01
CORIOLIS = 0.5
HEAT_COEF = 4.0
THIN_LIMIT = 0.1
FREEZING = -1.8
WARMTH_FACTOR = 0.05
STRESS_SCALE = 0.5

U, _, _, _, _, UO, VO, AREA, THICK, WX, WY, ICY = range(12)
NICE = 12
WET_ROW = WX
LANES = 128
TRACER_LANE = NICE * NSUB


def even(axis):
    return lax.rem(lax.axis_index(axis), 2) == 0


def spec(shape, index=None):
    zeros = (0,) * len(shape) if index is None else index
    return pl.BlockSpec(shape, lambda *_: zeros)


def vmem():
    return pl.BlockSpec(memory_space=pltpu.VMEM)


def pack_kernel(warm, salt, ocean, wind, ice, cover, volume, wet, icy, planes, inner, outer):
    levels, rows, _ = warm.shape
    for k in range(5):
        planes[U + k] = ice[k]
    planes[UO] = ocean[0]
    planes[VO] = ocean[1]
    planes[AREA] = cover[0] + cover[1] + cover[2] + cover[3] + cover[4]
    planes[THICK] = volume[0] + volume[1] + volume[2] + volume[3] + volume[4]
    planes[WX] = wind[0]
    planes[WY] = wind[1]
    planes[ICY] = icy[...].astype(jnp.float32)

    def eastward(out):
        for p in range(NICE):
            out[NSUB * p : NSUB * (p + 1), :] = planes[p, rows - NSUB :, :]
        at = NSUB * WET_ROW
        out[at : at + 1, :] = wet[rows - 1 :, :].astype(jnp.float32)
        out[NICE * NSUB : NICE * NSUB + levels, :] = warm[:, rows - 1, :]
        out[NICE * NSUB + levels :, :] = salt[:, rows - 1, :]

    def westward(out):
        for p in range(NICE):
            out[NSUB * p : NSUB * (p + 1), :] = planes[p, :NSUB, :]
        at = NSUB * WET_ROW + NSUB - 1
        out[at : at + 1, :] = wet[:1, :].astype(jnp.float32)
        out[NICE * NSUB : NICE * NSUB + levels, :] = warm[:, 0, :]
        out[NICE * NSUB + levels :, :] = salt[:, 0, :]

    @pl.when(even("grp"))
    def _():
        eastward(inner)
        westward(outer)

    @pl.when(jnp.logical_not(even("grp")))
    def _():
        westward(inner)
        eastward(outer)


def columns_kernel(warm, salt, wet, planes, inner, outer, edge, first, second):
    levels, rows, cols = warm.shape

    def place(east, west):
        for p in range(NICE):
            edge[p, :NSUB, :] = east[NSUB * p : NSUB * (p + 1), :]
            edge[p, NSUB:, :] = west[NSUB * p : NSUB * (p + 1), :]

    @pl.when(even("grp"))
    def _():
        place(inner, outer)

    @pl.when(jnp.logical_not(even("grp")))
    def _():
        place(outer, inner)

    def gathered(source, count):
        lane = lax.broadcasted_iota(jnp.int32, (count, LANES), 1)
        low = jnp.zeros((count, LANES), jnp.float32)
        high = low
        for p in range(NICE):
            here = (lane >= NSUB * p) & (lane < NSUB * (p + 1))
            low = jnp.where(here, pltpu.roll(source[p, :, :LANES], NSUB * p, 1), low)
            high = jnp.where(
                here, pltpu.roll(source[p, :, cols - LANES :], NSUB * (p + 1), 1), high
            )
        return lane, low, high

    lane, low, high = gathered(planes, rows)
    for p in range(2 * levels + 1):
        if p < levels:
            left, right = warm[p, :, :LANES], warm[p, :, cols - LANES :]
        elif p < 2 * levels:
            left, right = salt[p - levels, :, :LANES], salt[p - levels, :, cols - LANES :]
        else:
            left = wet[:, :LANES].astype(jnp.float32)
            right = wet[:, cols - LANES :].astype(jnp.float32)
        at = TRACER_LANE + p
        low = jnp.where(lane == at, pltpu.roll(left, at, 1), low)
        high = jnp.where(lane == at, pltpu.roll(right, at + 1, 1), high)
    _, low_edge, high_edge = gathered(edge, 2 * NSUB)
    north_first = even("gy")
    first[:rows, :] = jnp.where(north_first, high, low)
    first[rows:, :] = jnp.where(north_first, high_edge, low_edge)
    second[:rows, :] = jnp.where(north_first, low, high)
    second[rows:, :] = jnp.where(north_first, low_edge, high_edge)


def sides(first, second):
    north_first = even("gy")
    one, two = first[...], second[...]
    return jnp.where(north_first, two, one), jnp.where(north_first, one, two)


def columns_of(low, high, p):
    lane = lax.broadcasted_iota(jnp.int32, low.shape, 1)
    above = high if p == 0 else pltpu.roll(high, LANES - NSUB * p, 1)
    below = pltpu.roll(low, LANES - NSUB * (p + 1), 1)
    return jnp.where(lane < NSUB, above, jnp.where(lane >= LANES - NSUB, below, 0.0))


def ice_kernel(planes, edge, first, second, wet, home, velocity, picked):
    rows, cols = wet.shape
    pieces = cols // LANES
    tall = rows + 2 * NSUB
    broad = cols + LANES
    low, high = sides(first, second)
    wide = [
        jnp.concatenate(
            [jnp.concatenate([planes[p], edge[p]], axis=0), columns_of(low, high, p)], axis=1
        )
        for p in range(NICE)
    ]
    east = lambda f: pltpu.roll(f, tall - 1, 0)
    west = lambda f: pltpu.roll(f, 1, 0)
    north = lambda f: pltpu.roll(f, broad - 1, 1)
    south = lambda f: pltpu.roll(f, 1, 1)
    area, thick, mask = wide[AREA], wide[THICK], wide[ICY]
    strength = (thick * jnp.exp(-STRENGTH_COEF * (1.0 - area))) * RELAX_RATE
    mass = thick + MIN_MASS
    keep = mask * (1.0 / (1.0 + RELAX_RATE))
    ocean_u, ocean_v = wide[UO], wide[VO]
    u, v, s1, s2, s12 = (wide[k] for k in range(5))
    for _ in range(NSUB):
        du, dv = east(u) - u, north(v) - v
        div, ten = du + dv, du - dv
        shr = (north(u) - u) + (east(v) - v)
        visc = strength * lax.rsqrt(
            div * div + (ten * ten + shr * shr) * (1.0 / ECCENTRIC) + DELTA_FLOOR
        )
        quarter = visc * (1.0 / ECCENTRIC)
        s1 = keep * (s1 + (visc * div - strength))
        s2 = keep * (s2 + quarter * ten)
        s12 = keep * (s12 + quarter * shr)
        total, gap = s1 + s2, s1 - s2
        force_u = 0.5 * (total - west(total)) + (s12 - south(s12))
        force_v = 0.5 * (gap - south(gap)) + (s12 - west(s12))
        coef = area * jnp.sqrt((ocean_u - u) ** 2 + (ocean_v - v) ** 2 + SPEED_FLOOR)
        scale = mask / (mass + coef)
        turn = CORIOLIS * mass
        u, v = (
            scale * (mass * u + force_u + wide[WX] + coef * ocean_u + turn * v),
            scale * (mass * v + force_v + wide[WY] + coef * ocean_v - turn * u),
        )
    own = lambda f: f[:rows, :cols]
    u, v, ocean_u, ocean_v = own(u), own(v), own(ocean_u), own(ocean_v)
    coef = own(area) * jnp.sqrt((ocean_u - u) ** 2 + (ocean_v - v) ** 2 + SPEED_FLOOR)
    drag = (STRESS_SCALE * own(mask)) * coef
    sea = wet[...].astype(jnp.float32)
    velocity[0] = sea * (ocean_u + drag * (u - ocean_u))
    velocity[1] = sea * (ocean_v + drag * (v - ocean_v))
    for k, f in enumerate((u, v, own(s1), own(s2), own(s12))):
        blocks = [f[:, LANES * b : LANES * (b + 1)] for b in range(pieces)]
        for owner in range(pieces):
            value = jnp.zeros_like(blocks[0])
            for b in range(pieces):
                value = jnp.where(home[0, b] == owner, blocks[b], value)
            picked[owner, k] = value


def tracer_kernel(
    warm, salt, wet, icy, cover, volume, first, second, inner, outer,
    warm_out, salt_out, coef, cut_low, cut_high, gain, rise,
):
    step = pl.program_id(0)
    levels, rows, cols = warm.shape
    count = warm_out.shape[0]
    low, high = sides(first, second)
    low, high = low[:rows], high[:rows]
    top = NICE * NSUB

    @pl.when(step == 0)
    def _():
        lane = lax.broadcasted_iota(jnp.int32, (rows, cols), 1)
        row = lax.broadcasted_iota(jnp.int32, (rows, cols), 0)
        short = lax.broadcasted_iota(jnp.int32, (rows, LANES), 1)
        sea = wet[...].astype(jnp.float32)
        mine = DIFFUSIVITY * sea
        east = jnp.where(row < rows - 1, mine * pltpu.roll(sea, rows - 1, 0), 0.0)
        west = jnp.where(row > 0, mine * pltpu.roll(sea, 1, 0), 0.0)
        north = jnp.where(lane < cols - 1, mine * pltpu.roll(sea, cols - 1, 1), 0.0)
        south = jnp.where(lane > 0, mine * pltpu.roll(sea, 1, 1), 0.0)
        at = TRACER_LANE + 2 * levels
        edge_low = jnp.where(short == 0, mine[:, :LANES] * pltpu.roll(low, LANES - at, 1), 0.0)
        edge_high = jnp.where(
            short == LANES - 1,
            mine[:, cols - LANES :] * pltpu.roll(high, LANES - 1 - at, 1),
            0.0,
        )
        coef[1], coef[2], coef[3], coef[4] = east, west, north, south
        coef[0] = 1.0 - (east + west + north + south)
        coef[0, :, :LANES] -= edge_low
        coef[0, :, cols - LANES :] -= edge_high
        cut_low[...], cut_high[...] = edge_low, edge_high
        last, head = NSUB * WET_ROW + NSUB - 1, NSUB * WET_ROW

        def fluxes(from_east, from_west):
            east_gain = mine[rows - 1 :, :] * from_east[last : last + 1, :]
            west_gain = mine[:1, :] * from_west[head : head + 1, :]
            coef[0, rows - 1 :, :] -= east_gain
            coef[0, :1, :] -= west_gain
            rise[...] = east_gain * from_east[top:, :]
            gain[...] = west_gain * from_west[top:, :]

        @pl.when(even("grp"))
        def _():
            fluxes(inner, outer)

        @pl.when(jnp.logical_not(even("grp")))
        def _():
            fluxes(outer, inner)

    for part, (field, out) in enumerate(((warm, warm_out), (salt, salt_out))):
        for k in range(count):
            level = step * count + k
            f = field[level]
            out[k] = (
                coef[0] * f
                + coef[1] * pltpu.roll(f, rows - 1, 0)
                + coef[2] * pltpu.roll(f, 1, 0)
                + coef[3] * pltpu.roll(f, cols - 1, 1)
                + coef[4] * pltpu.roll(f, 1, 1)
            )
            plane = part * levels + level
            at = TRACER_LANE + plane
            out[k, :, :LANES] += cut_low[...] * pltpu.roll(low, LANES - at, 1)
            out[k, :, cols - LANES :] += cut_high[...] * pltpu.roll(high, LANES - 1 - at, 1)
            out[k, rows - 1 :, :] += rise[pl.ds(plane, 1), :]
            out[k, :1, :] += gain[pl.ds(plane, 1), :]

    @pl.when(step == 0)
    def _():
        heat = jnp.zeros((rows, cols), jnp.float32)
        for k in range(cover.shape[0]):
            heat += HEAT_COEF * cover[k] * cover[k] / (volume[k] + THIN_LIMIT * cover[k])
        heat *= icy[...].astype(jnp.float32) * (warm[0] - FREEZING)
        warm_out[0] -= WARMTH_FACTOR * wet[...].astype(jnp.float32) * heat


def place_kernel(pieces, out):
    for y in range(pieces.shape[0]):
        out[:, :, LANES * y : LANES * (y + 1)] = pieces[y]


def float_like(*shape):
    return jax.ShapeDtypeStruct(shape, jnp.float32)


def near(*shape):
    return pltpu.VMEM(shape, jnp.float32)


def held(*arrays):
    return tuple(pltpu.with_memory_space_constraint(a, pltpu.VMEM) for a in arrays)


def per_device(
    warm, salt, ocean, wind, ice, cover, volume, wet, icy, home
):
    levels, rows, cols = warm.shape
    grp, gy = lax.axis_size("grp"), lax.axis_size("gy")
    assert grp % 2 == 0 and gy % 2 == 0 and cols == gy * LANES
    swap = lambda pairs: [p for i, j in pairs for p in ((i, j), (j, i))]
    inner_pairs = swap([(i, i + 1) for i in range(0, grp, 2)])
    outer_pairs = swap([(i, (i + 1) % grp) for i in range(1, grp, 2)])
    first_pairs = swap([(i, i + 1) for i in range(0, gy, 2)])
    second_pairs = swap([(i, i + 1) for i in range(1, gy - 1, 2)])
    tall = rows + 2 * NSUB
    tile = near(tall, LANES)
    message = near(NICE * NSUB + 2 * levels, cols)


    planes, inner, outer = pl.pallas_call(
        pack_kernel,
        out_shape=[near(NICE, rows, cols), message, message],
        in_specs=[vmem()] * 9,
        out_specs=[vmem()] * 3,
        name="pack",
    )(warm, salt, ocean, wind, ice, cover, volume, wet, icy)
    outer = lax.ppermute(outer, "grp", outer_pairs)
    inner = lax.ppermute(inner, "grp", inner_pairs)

    edge, first, second = pl.pallas_call(
        columns_kernel,
        out_shape=[near(NICE, 2 * NSUB, cols), tile, tile],
        in_specs=[vmem()] * 6,
        out_specs=[vmem()] * 3,
        name="columns",
    )(warm, salt, wet, *held(planes, inner, outer))
    first = lax.ppermute(first, "gy", first_pairs)
    second = lax.ppermute(second, "gy", second_pairs)

    velocity, picked = pl.pallas_call(
        ice_kernel,
        out_shape=[float_like(2, rows, cols), float_like(gy, 5, rows, LANES)],
        in_specs=[vmem()] * 5 + [pl.BlockSpec(memory_space=pltpu.SMEM)],
        out_specs=[vmem()] * 2,
        name="ice",
    )(*held(planes, edge, first, second), wet, home)
    owned = lax.all_to_all(picked, "gy", split_axis=0, concat_axis=0, tiled=True)

    steps = 4
    block = pl.BlockSpec((levels // steps, rows, cols), lambda i: (i, 0, 0))
    warm_out, salt_out = pl.pallas_call(
        tracer_kernel,
        grid=(steps,),
        in_specs=[
            vmem(), vmem(), spec(wet.shape), spec(icy.shape), spec(cover.shape), spec(volume.shape),
            vmem(), vmem(), vmem(), vmem(),
        ],
        out_specs=[block, block],
        out_shape=[float_like(*warm.shape), float_like(*salt.shape)],
        scratch_shapes=[
            pltpu.VMEM((5, rows, cols), jnp.float32),
            pltpu.VMEM((rows, LANES), jnp.float32),
            pltpu.VMEM((rows, LANES), jnp.float32),
            pltpu.VMEM((2 * levels, cols), jnp.float32),
            pltpu.VMEM((2 * levels, cols), jnp.float32),
        ],
        name="tracers",
    )(warm, salt, wet, icy, cover, volume, *held(first, second, inner, outer))

    patch = pl.pallas_call(
        place_kernel,
        out_shape=float_like(5, rows, cols),
        in_specs=[vmem()],
        out_specs=vmem(),
        name="place",
    )(*held(owned))
    return warm_out, salt_out, velocity, patch


def solution(mesh):
    field = P(None, "grp", "gy")
    flat = P("grp", "gy")

    return jax.shard_map(
        per_device,
        mesh=mesh,
        in_specs=(field,) * 7 + (flat,) * 3,
        out_specs=(field,) * 4,
        check_vma=False,
    )
```

```python
import jax
import jax.numpy as jnp
from jax import lax
from jax.experimental import pallas as pl
from jax.experimental.pallas import tpu as pltpu
from jax.sharding import PartitionSpec as P


NSUB = 4
DIFFUSIVITY = 0.2
STRENGTH_COEF = 20.0
MIN_MASS = 0.5
RELAX_RATE = 0.5
ECCENTRIC = 4.0
DELTA_FLOOR = 0.0025
SPEED_FLOOR = 0.01
CORIOLIS = 0.5
HEAT_COEF = 4.0
THIN_LIMIT = 0.1
FREEZING = -1.8
WARMTH_FACTOR = 0.05
STRESS_SCALE = 0.5

U, _, _, _, _, UO, VO, AREA, THICK, WX, WY, ICY = range(12)
NICE = 12
WET_ROW = WX
LANES = 128
TRACER_LANE = NICE * NSUB


def even(axis):
    return lax.rem(lax.axis_index(axis), 2) == 0


def spec(shape, index=None):
    zeros = (0,) * len(shape) if index is None else index
    return pl.BlockSpec(shape, lambda *_: zeros)


def vmem():
    return pl.BlockSpec(memory_space=pltpu.VMEM)


def outer_kernel(*refs):
    fields, warm, salt, out = refs[:7], refs[7], refs[8], refs[9]
    tiles, sems, row_sems = refs[10:17], refs[17], refs[18]
    levels, rows, _ = warm.shape
    half = rows // 2
    top = NICE * NSUB

    def message(start, row, wet_slot, edge_row):
        copies = [
            pltpu.make_async_copy(f.at[..., start : start + half, :], tile, sems.at[k])
            for k, (f, tile) in enumerate(zip(fields, tiles))
        ]
        lines = [
            pltpu.make_async_copy(
                f.at[:, start + edge_row, :], out.at[top + k * levels : top + (k + 1) * levels, :], row_sems.at[k]
            )
            for k, f in enumerate((warm, salt))
        ]
        for copy in copies + lines:
            copy.start()
        for copy in copies:
            copy.wait()
        ocean, wind, ice, cover, volume, wet, icy = tiles
        cut = slice(row, row + NSUB)
        planes = [ice[k, cut, :] for k in range(5)] + [ocean[0, cut, :], ocean[1, cut, :]]
        planes += [sum(f[k, cut, :] for k in range(f.shape[0])) for f in (cover, volume)]
        planes += [wind[0, cut, :], wind[1, cut, :], icy[cut, :].astype(jnp.float32)]
        for p in range(NICE):
            out[NSUB * p : NSUB * (p + 1), :] = planes[p]
        at = NSUB * WET_ROW + wet_slot
        out[at : at + 1, :] = wet[edge_row : edge_row + 1, :].astype(jnp.float32)
        for copy in lines:
            copy.wait()

    @pl.when(even("grp"))
    def _():
        message(0, 0, NSUB - 1, 0)

    @pl.when(jnp.logical_not(even("grp")))
    def _():
        message(half, half - NSUB, 0, half - 1)


def gathered(source, count):
    cols = source.shape[2]
    lane = lax.broadcasted_iota(jnp.int32, (count, LANES), 1)
    low = jnp.zeros((count, LANES), jnp.float32)
    high = low
    for p in range(NICE):
        here = (lane >= NSUB * p) & (lane < NSUB * (p + 1))
        low = jnp.where(here, pltpu.roll(source[p, :, :LANES], NSUB * p, 1), low)
        high = jnp.where(here, pltpu.roll(source[p, :, cols - LANES :], NSUB * (p + 1), 1), high)
    return lane, low, high


def inner_kernel(
    warm, salt, ocean, wind, ice, cover, volume, wet, icy, home,
    planes, inner, low_out, high_out, sea, chosen,
):
    levels, rows, cols = warm.shape
    for k in range(5):
        planes[U + k] = ice[k]
    planes[UO] = ocean[0]
    planes[VO] = ocean[1]
    planes[AREA] = sum(cover[k] for k in range(cover.shape[0]))
    planes[THICK] = sum(volume[k] for k in range(volume.shape[0]))
    planes[WX] = wind[0]
    planes[WY] = wind[1]
    planes[ICY] = icy[...].astype(jnp.float32)
    sea[...] = wet[...].astype(jnp.float32)
    blocks = home.shape[1]
    for owner in range(blocks):
        for b in range(blocks):
            flag = jnp.where(home[0, b] == owner, 1.0, 0.0)
            chosen[owner * blocks + b] = jnp.full(chosen.shape[1:], flag, jnp.float32)

    def message(row, wet_slot, edge_row):
        for p in range(NICE):
            inner[NSUB * p : NSUB * (p + 1), :] = planes[p, row : row + NSUB, :]
        at = NSUB * WET_ROW + wet_slot
        inner[at : at + 1, :] = sea[edge_row : edge_row + 1, :]
        inner[NICE * NSUB : NICE * NSUB + levels, :] = warm[:, edge_row, :]
        inner[NICE * NSUB + levels :, :] = salt[:, edge_row, :]

    @pl.when(even("grp"))
    def _():
        message(rows - NSUB, 0, rows - 1)

    @pl.when(jnp.logical_not(even("grp")))
    def _():
        message(0, NSUB - 1, 0)

    lane, low, high = gathered(planes, rows)
    for p in range(2 * levels + 1):
        if p < 2 * levels:
            field = warm[p] if p < levels else salt[p - levels]
        else:
            field = sea[...]
        at = TRACER_LANE + p
        low = jnp.where(lane == at, pltpu.roll(field[:, :LANES], at, 1), low)
        high = jnp.where(lane == at, pltpu.roll(field[:, cols - LANES :], at + 1, 1), high)
    low_out[...] = low
    high_out[...] = high


def edge_kernel(inner, outer, low, high, edge, first, second):
    rows = low.shape[0]

    def place(east, west):
        for p in range(NICE):
            edge[p, :NSUB, :] = east[NSUB * p : NSUB * (p + 1), :]
            edge[p, NSUB:, :] = west[NSUB * p : NSUB * (p + 1), :]

    @pl.when(even("grp"))
    def _():
        place(inner, outer)

    @pl.when(jnp.logical_not(even("grp")))
    def _():
        place(outer, inner)

    _, low_edge, high_edge = gathered(edge, 2 * NSUB)
    north_first = even("gy")
    first[:rows, :] = jnp.where(north_first, high[...], low[...])
    first[rows:, :] = jnp.where(north_first, high_edge, low_edge)
    second[:rows, :] = jnp.where(north_first, low[...], high[...])
    second[rows:, :] = jnp.where(north_first, low_edge, high_edge)


def sides(first, second):
    north_first = even("gy")
    one, two = first[...], second[...]
    return jnp.where(north_first, two, one), jnp.where(north_first, one, two)


def columns_of(low, high, p):
    lane = lax.broadcasted_iota(jnp.int32, low.shape, 1)
    above = high if p == 0 else pltpu.roll(high, LANES - NSUB * p, 1)
    below = pltpu.roll(low, LANES - NSUB * (p + 1), 1)
    return jnp.where(lane < NSUB, above, jnp.where(lane >= LANES - NSUB, below, 0.0))


def root(square):
    return square * lax.rsqrt(square)


def ice_kernel(planes, edge, first, second, sea, chosen, velocity, picked):
    rows, cols = sea.shape
    pieces = cols // LANES
    tall = rows + 2 * NSUB
    broad = cols + LANES
    low, high = sides(first, second)
    wide = [
        jnp.concatenate(
            [jnp.concatenate([planes[p], edge[p]], axis=0), columns_of(low, high, p)], axis=1
        )
        for p in range(NICE)
    ]
    east = lambda f: pltpu.roll(f, tall - 1, 0)
    west = lambda f: pltpu.roll(f, 1, 0)
    north = lambda f: pltpu.roll(f, broad - 1, 1)
    south = lambda f: pltpu.roll(f, 1, 1)
    area, thick, mask = wide[AREA], wide[THICK], wide[ICY]
    strength = (thick * jnp.exp(-STRENGTH_COEF * (1.0 - area))) * RELAX_RATE
    mass = thick + MIN_MASS
    keep = mask * (1.0 / (1.0 + RELAX_RATE))
    ocean_u, ocean_v = wide[UO], wide[VO]
    u, v, s1, s2, s12 = (wide[k] for k in range(5))
    for _ in range(NSUB):
        du, dv = east(u) - u, north(v) - v
        div, ten = du + dv, du - dv
        shr = (north(u) - u) + (east(v) - v)
        visc = strength * lax.rsqrt(
            div * div + (ten * ten + shr * shr) * (1.0 / ECCENTRIC) + DELTA_FLOOR
        )
        quarter = visc * (1.0 / ECCENTRIC)
        s1 = keep * (s1 + (visc * div - strength))
        s2 = keep * (s2 + quarter * ten)
        s12 = keep * (s12 + quarter * shr)
        total, gap = s1 + s2, s1 - s2
        force_u = 0.5 * (total - west(total)) + (s12 - south(s12))
        force_v = 0.5 * (gap - south(gap)) + (s12 - west(s12))
        coef = area * root((ocean_u - u) ** 2 + (ocean_v - v) ** 2 + SPEED_FLOOR)
        scale = mask / (mass + coef)
        turn = CORIOLIS * mass
        u, v = (
            scale * (mass * u + force_u + wide[WX] + coef * ocean_u + turn * v),
            scale * (mass * v + force_v + wide[WY] + coef * ocean_v - turn * u),
        )
    own = lambda f: f[:rows, :cols]
    u, v, ocean_u, ocean_v = own(u), own(v), own(ocean_u), own(ocean_v)
    coef = own(area) * root((ocean_u - u) ** 2 + (ocean_v - v) ** 2 + SPEED_FLOOR)
    drag = (STRESS_SCALE * own(mask)) * coef
    velocity[0] = sea[...] * (ocean_u + drag * (u - ocean_u))
    velocity[1] = sea[...] * (ocean_v + drag * (v - ocean_v))
    here = [jnp.concatenate([chosen[k]] * (rows // 8), axis=0) > 0.5 for k in range(pieces * pieces)]
    for k, f in enumerate((u, v, own(s1), own(s2), own(s12))):
        blocks = [f[:, LANES * b : LANES * (b + 1)] for b in range(pieces)]
        for owner in range(pieces):
            value = jnp.zeros_like(blocks[0])
            for b in range(pieces):
                value = jnp.where(here[owner * pieces + b], blocks[b], value)
            picked[owner, k] = value


def tracer_kernel(
    warm, salt, sea_in, icy, cover, volume, first, second, inner, outer, flow,
    warm_out, salt_out, flow_out, coef, cut_low, cut_high, gain, rise,
):
    step = pl.program_id(0)
    levels, rows, cols = warm.shape
    count = warm_out.shape[0]
    low, high = sides(first, second)
    low, high = low[:rows], high[:rows]
    top = NICE * NSUB

    @pl.when(step == 0)
    def _():
        lane = lax.broadcasted_iota(jnp.int32, (rows, cols), 1)
        row = lax.broadcasted_iota(jnp.int32, (rows, cols), 0)
        short = lax.broadcasted_iota(jnp.int32, (rows, LANES), 1)
        flow_out[...] = flow[...]
        sea = sea_in[...]
        mine = DIFFUSIVITY * sea
        east = jnp.where(row < rows - 1, mine * pltpu.roll(sea, rows - 1, 0), 0.0)
        west = jnp.where(row > 0, mine * pltpu.roll(sea, 1, 0), 0.0)
        north = jnp.where(lane < cols - 1, mine * pltpu.roll(sea, cols - 1, 1), 0.0)
        south = jnp.where(lane > 0, mine * pltpu.roll(sea, 1, 1), 0.0)
        at = TRACER_LANE + 2 * levels
        edge_low = jnp.where(short == 0, mine[:, :LANES] * pltpu.roll(low, LANES - at, 1), 0.0)
        edge_high = jnp.where(
            short == LANES - 1,
            mine[:, cols - LANES :] * pltpu.roll(high, LANES - 1 - at, 1),
            0.0,
        )
        coef[1], coef[2], coef[3], coef[4] = east, west, north, south
        coef[0] = 1.0 - (east + west + north + south)
        coef[0, :, :LANES] -= edge_low
        coef[0, :, cols - LANES :] -= edge_high
        cut_low[...], cut_high[...] = edge_low, edge_high
        last, head = NSUB * WET_ROW + NSUB - 1, NSUB * WET_ROW

        def fluxes(from_east, from_west):
            east_gain = mine[rows - 1 :, :] * from_east[last : last + 1, :]
            west_gain = mine[:1, :] * from_west[head : head + 1, :]
            coef[0, rows - 1 :, :] -= east_gain
            coef[0, :1, :] -= west_gain
            rise[...] = east_gain * from_east[top:, :]
            gain[...] = west_gain * from_west[top:, :]

        @pl.when(even("grp"))
        def _():
            fluxes(inner, outer)

        @pl.when(jnp.logical_not(even("grp")))
        def _():
            fluxes(outer, inner)

    for part, (field, out) in enumerate(((warm, warm_out), (salt, salt_out))):
        for k in range(count):
            level = step * count + k
            f = field[level]
            out[k] = (
                coef[0] * f
                + coef[1] * pltpu.roll(f, rows - 1, 0)
                + coef[2] * pltpu.roll(f, 1, 0)
                + coef[3] * pltpu.roll(f, cols - 1, 1)
                + coef[4] * pltpu.roll(f, 1, 1)
            )
            plane = part * levels + level
            at = TRACER_LANE + plane
            out[k, :, :LANES] += cut_low[...] * pltpu.roll(low, LANES - at, 1)
            out[k, :, cols - LANES :] += cut_high[...] * pltpu.roll(high, LANES - 1 - at, 1)
            out[k, rows - 1 :, :] += rise[pl.ds(plane, 1), :]
            out[k, :1, :] += gain[pl.ds(plane, 1), :]

    @pl.when(step == 0)
    def _():
        heat = jnp.zeros((rows, cols), jnp.float32)
        for k in range(cover.shape[0]):
            heat += HEAT_COEF * cover[k] * cover[k] / (volume[k] + THIN_LIMIT * cover[k])
        heat *= icy[...].astype(jnp.float32) * (warm[0] - FREEZING)
        warm_out[0] -= WARMTH_FACTOR * sea_in[...] * heat


def place_kernel(pieces, out, sems):
    copies = [
        pltpu.make_async_copy(pieces.at[y], out.at[:, :, LANES * y : LANES * (y + 1)], sems.at[y])
        for y in range(pieces.shape[0])
    ]
    for copy in copies:
        copy.start()
    for copy in copies:
        copy.wait()


def float_like(*shape):
    return jax.ShapeDtypeStruct(shape, jnp.float32)


def near(*shape):
    return pltpu.VMEM(shape, jnp.float32)


def held(*arrays):
    return tuple(pltpu.with_memory_space_constraint(a, pltpu.VMEM) for a in arrays)


def per_device(
    warm, salt, ocean, wind, ice, cover, volume, wet, icy, home
):
    levels, rows, cols = warm.shape
    grp, gy = lax.axis_size("grp"), lax.axis_size("gy")
    assert grp % 2 == 0 and gy % 2 == 0 and cols == gy * LANES
    swap = lambda pairs: [p for i, j in pairs for p in ((i, j), (j, i))]
    inner_pairs = swap([(i, i + 1) for i in range(0, grp, 2)])
    outer_pairs = swap([(i, (i + 1) % grp) for i in range(1, grp, 2)])
    first_pairs = swap([(i, i + 1) for i in range(0, gy, 2)])
    second_pairs = swap([(i, i + 1) for i in range(1, gy - 1, 2)])
    tall = rows + 2 * NSUB
    tile = near(tall, LANES)
    message = near(NICE * NSUB + 2 * levels, cols)


    sources = (warm, salt, ocean, wind, ice, cover, volume, wet, icy)
    half = lambda a: a.shape[:-2] + (rows // 2, cols)
    anywhere = pl.BlockSpec(memory_space=pl.ANY)
    outer = pl.pallas_call(
        outer_kernel,
        out_shape=message,
        in_specs=[anywhere] * len(sources),
        out_specs=vmem(),
        scratch_shapes=[pltpu.VMEM(half(a), a.dtype) for a in sources[2:]]
        + [pltpu.SemaphoreType.DMA((len(sources) - 2,)), pltpu.SemaphoreType.DMA((2,))],
        name="outer_pack",
    )(*sources[2:], warm, salt)
    outer = lax.ppermute(outer, "grp", outer_pairs)
    blocks = home.shape[1]
    own = near(rows, LANES)
    planes, inner, low, high, sea, chosen = pl.pallas_call(
        inner_kernel,
        out_shape=[
            near(NICE, rows, cols), message, own, own, near(rows, cols), near(blocks * blocks, 8, LANES),
        ],
        in_specs=[vmem()] * 9 + [pl.BlockSpec(memory_space=pltpu.SMEM)],
        out_specs=[vmem()] * 6,
        name="inner_pack",
    )(*sources, home)
    inner = lax.ppermute(inner, "grp", inner_pairs)

    edge, first, second = pl.pallas_call(
        edge_kernel,
        out_shape=[near(NICE, 2 * NSUB, cols), tile, tile],
        in_specs=[vmem()] * 4,
        out_specs=[vmem()] * 3,
        name="edge",
    )(*held(inner, outer, low, high))
    second = lax.ppermute(second, "gy", second_pairs)
    first = lax.ppermute(first, "gy", first_pairs)

    velocity, picked = pl.pallas_call(
        ice_kernel,
        out_shape=[near(2, rows, cols), float_like(gy, 5, rows, LANES)],
        in_specs=[vmem()] * 6,
        out_specs=[vmem()] * 2,
        name="ice",
    )(*held(planes, edge, first, second, sea, chosen))
    owned = lax.all_to_all(picked, "gy", split_axis=0, concat_axis=0, tiled=True)

    steps = 4
    block = pl.BlockSpec((levels // steps, rows, cols), lambda i: (i, 0, 0))
    warm_out, salt_out, velocity = pl.pallas_call(
        tracer_kernel,
        grid=(steps,),
        in_specs=[
            vmem(), vmem(), vmem(), spec(icy.shape), spec(cover.shape), spec(volume.shape),
            vmem(), vmem(), vmem(), vmem(), vmem(),
        ],
        out_specs=[block, block, spec(ocean.shape)],
        out_shape=[float_like(*warm.shape), float_like(*salt.shape), float_like(*ocean.shape)],
        scratch_shapes=[
            pltpu.VMEM((5, rows, cols), jnp.float32),
            pltpu.VMEM((rows, LANES), jnp.float32),
            pltpu.VMEM((rows, LANES), jnp.float32),
            pltpu.VMEM((2 * levels, cols), jnp.float32),
            pltpu.VMEM((2 * levels, cols), jnp.float32),
        ],
        name="tracers",
    )(warm, salt, *held(sea), icy, cover, volume, *held(first, second, inner, outer, velocity))

    patch = pl.pallas_call(
        place_kernel,
        out_shape=float_like(5, rows, cols),
        in_specs=[vmem()],
        out_specs=anywhere,
        scratch_shapes=[pltpu.SemaphoreType.DMA((gy,))],
        name="place",
    )(*held(owned))
    return warm_out, salt_out, velocity, patch


def solution(mesh):
    field = P(None, "grp", "gy")
    flat = P("grp", "gy")

    return jax.shard_map(
        per_device,
        mesh=mesh,
        in_specs=(field,) * 7 + (flat,) * 3,
        out_specs=(field,) * 4,
        check_vma=False,
    )
```

```python
import jax
import jax.numpy as jnp
from jax import lax
from jax.experimental import pallas as pl
from jax.experimental.pallas import tpu as pltpu
from jax.sharding import PartitionSpec as P


NSUB = 4
DIFFUSIVITY = 0.2
STRENGTH_COEF = 20.0
MIN_MASS = 0.5
RELAX_RATE = 0.5
ECCENTRIC = 4.0
DELTA_FLOOR = 0.0025
SPEED_FLOOR = 0.01
CORIOLIS = 0.5
HEAT_COEF = 4.0
THIN_LIMIT = 0.1
FREEZING = -1.8
WARMTH_FACTOR = 0.05
STRESS_SCALE = 0.5

U, _, _, _, _, UO, VO, AREA, THICK, WX, WY, ICY = range(12)
NICE = 12
WET_ROW = WX
LANES = 128
REACH = 2 * NSUB
FLOW_LANE, HOME_LANE = 32, 64


def even(axis):
    return lax.rem(lax.axis_index(axis), 2) == 0


def spec(shape, index=None):
    zeros = (0,) * len(shape) if index is None else index
    return pl.BlockSpec(shape, lambda *_: zeros)


def vmem():
    return pl.BlockSpec(memory_space=pltpu.VMEM)


def outer_kernel(*refs):
    fields, warm, salt, out = refs[:7], refs[7], refs[8], refs[9]
    tiles, sems, row_sems = refs[10:17], refs[17], refs[18]
    levels, rows, _ = warm.shape
    half = rows // 2
    top = NICE * NSUB

    def message(start, row, wet_slot, edge_row):
        copies = [
            pltpu.make_async_copy(f.at[..., start : start + half, :], tile, sems.at[k])
            for k, (f, tile) in enumerate(zip(fields, tiles))
        ]
        lines = [
            pltpu.make_async_copy(
                f.at[:, start + edge_row, :], out.at[top + k * levels : top + (k + 1) * levels, :], row_sems.at[k]
            )
            for k, f in enumerate((warm, salt))
        ]
        for copy in copies + lines:
            copy.start()
        for copy in copies:
            copy.wait()
        ocean, wind, ice, cover, volume, wet, icy = tiles
        cut = slice(row, row + NSUB)
        planes = [ice[k, cut, :] for k in range(5)] + [ocean[0, cut, :], ocean[1, cut, :]]
        planes += [sum(f[k, cut, :] for k in range(f.shape[0])) for f in (cover, volume)]
        planes += [wind[0, cut, :], wind[1, cut, :], icy[cut, :].astype(jnp.float32)]
        for p in range(NICE):
            out[NSUB * p : NSUB * (p + 1), :] = planes[p]
        at = NSUB * WET_ROW + wet_slot
        out[at : at + 1, :] = wet[edge_row : edge_row + 1, :].astype(jnp.float32)
        for copy in lines:
            copy.wait()

    @pl.when(even("grp"))
    def _():
        message(0, 0, NSUB - 1, 0)

    @pl.when(jnp.logical_not(even("grp")))
    def _():
        message(half, half - NSUB, 0, half - 1)


def gathered(source, count):
    lane = lax.broadcasted_iota(jnp.int32, (count, LANES), 1)
    tile = jnp.zeros((count, LANES), jnp.float32)
    for p in range(NICE):
        here = (lane >= REACH * p) & (lane < REACH * (p + 1))
        tile = jnp.where(here, pltpu.roll(source[p, :, :LANES], REACH * p, 1), tile)
    return tile


def inner_kernel(
    warm, salt, ocean, wind, ice, cover, volume, wet, icy, home,
    planes, inner, own, down, up, sea, chosen,
):
    levels, rows, cols = warm.shape
    for k in range(5):
        planes[U + k] = ice[k]
    planes[UO] = ocean[0]
    planes[VO] = ocean[1]
    planes[AREA] = sum(cover[k] for k in range(cover.shape[0]))
    planes[THICK] = sum(volume[k] for k in range(volume.shape[0]))
    planes[WX] = wind[0]
    planes[WY] = wind[1]
    planes[ICY] = icy[...].astype(jnp.float32)
    sea[...] = wet[...].astype(jnp.float32)
    blocks = home.shape[1]
    for owner in range(blocks):
        for b in range(blocks):
            flag = jnp.where(home[0, b] == owner, 1.0, 0.0)
            chosen[owner * blocks + b] = jnp.full(chosen.shape[1:], flag, jnp.float32)

    def message(row, wet_slot, edge_row):
        for p in range(NICE):
            inner[NSUB * p : NSUB * (p + 1), :] = planes[p, row : row + NSUB, :]
        at = NSUB * WET_ROW + wet_slot
        inner[at : at + 1, :] = sea[edge_row : edge_row + 1, :]
        inner[NICE * NSUB : NICE * NSUB + levels, :] = warm[:, edge_row, :]
        inner[NICE * NSUB + levels :, :] = salt[:, edge_row, :]

    @pl.when(even("grp"))
    def _():
        message(rows - NSUB, 0, rows - 1)

    @pl.when(jnp.logical_not(even("grp")))
    def _():
        message(0, NSUB - 1, 0)

    own[...] = gathered(planes, rows)
    lane = lax.broadcasted_iota(jnp.int32, (rows, LANES), 1)
    first_home = home[0, 0].astype(jnp.float32)
    low = jnp.where((lane >= HOME_LANE) & (lane < HOME_LANE + NSUB), first_home, 0.0)
    high = jnp.zeros((rows, LANES), jnp.float32)
    for p in range(2 * levels + 1):
        if p < 2 * levels:
            field = warm[p] if p < levels else salt[p - levels]
        else:
            field = sea[...]
        low = jnp.where(lane == p, pltpu.roll(field[:, :LANES], p, 1), low)
        high = jnp.where(lane == p, pltpu.roll(field[:, cols - LANES :], p + 1, 1), high)
    down[...] = low
    up[...] = high


def edge_kernel(inner, outer, own, tracer, edge, down):
    rows = own.shape[0]

    def place(east, west):
        for p in range(NICE):
            edge[p, :NSUB, :] = east[NSUB * p : NSUB * (p + 1), :]
            edge[p, NSUB:, :] = west[NSUB * p : NSUB * (p + 1), :]

    @pl.when(even("grp"))
    def _():
        place(inner, outer)

    @pl.when(jnp.logical_not(even("grp")))
    def _():
        place(outer, inner)

    tall = rows + 2 * NSUB
    down[:rows, :] = own[...]
    down[rows:tall, :] = gathered(edge, 2 * NSUB)
    down[tall:, :] = tracer[...]


def columns_of(tile, p):
    lane = lax.broadcasted_iota(jnp.int32, tile.shape, 1)
    return jnp.where(lane < REACH, tile if p == 0 else pltpu.roll(tile, LANES - REACH * p, 1), 0.0)


def root(square):
    return square * lax.rsqrt(square)


def ice_kernel(planes, edge, down, sea, chosen, velocity, picked):
    rows, cols = sea.shape
    pieces = cols // LANES
    tall = rows + 2 * NSUB
    broad = cols + LANES
    tile = down[:tall, :]
    wide = [
        jnp.concatenate(
            [jnp.concatenate([planes[p], edge[p]], axis=0), columns_of(tile, p)], axis=1
        )
        for p in range(NICE)
    ]
    east = lambda f: pltpu.roll(f, tall - 1, 0)
    west = lambda f: pltpu.roll(f, 1, 0)
    north = lambda f: pltpu.roll(f, broad - 1, 1)
    south = lambda f: pltpu.roll(f, 1, 1)
    area, thick, mask = wide[AREA], wide[THICK], wide[ICY]
    strength = (thick * jnp.exp(-STRENGTH_COEF * (1.0 - area))) * RELAX_RATE
    mass = thick + MIN_MASS
    keep = mask * (1.0 / (1.0 + RELAX_RATE))
    ocean_u, ocean_v = wide[UO], wide[VO]
    u, v, s1, s2, s12 = (wide[k] for k in range(5))
    for _ in range(NSUB):
        du, dv = east(u) - u, north(v) - v
        div, ten = du + dv, du - dv
        shr = (north(u) - u) + (east(v) - v)
        visc = strength * lax.rsqrt(
            div * div + (ten * ten + shr * shr) * (1.0 / ECCENTRIC) + DELTA_FLOOR
        )
        quarter = visc * (1.0 / ECCENTRIC)
        s1 = keep * (s1 + (visc * div - strength))
        s2 = keep * (s2 + quarter * ten)
        s12 = keep * (s12 + quarter * shr)
        total, gap = s1 + s2, s1 - s2
        force_u = 0.5 * (total - west(total)) + (s12 - south(s12))
        force_v = 0.5 * (gap - south(gap)) + (s12 - west(s12))
        coef = area * root((ocean_u - u) ** 2 + (ocean_v - v) ** 2 + SPEED_FLOOR)
        scale = mask / (mass + coef)
        turn = CORIOLIS * mass
        u, v = (
            scale * (mass * u + force_u + wide[WX] + coef * ocean_u + turn * v),
            scale * (mass * v + force_v + wide[WY] + coef * ocean_v - turn * u),
        )
    own = lambda f: f[:rows, :]
    u, v, s1, s2, s12, ocean_u, ocean_v = (own(f) for f in (u, v, s1, s2, s12, ocean_u, ocean_v))
    coef = own(area) * root((ocean_u - u) ** 2 + (ocean_v - v) ** 2 + SPEED_FLOOR)
    drag = (STRESS_SCALE * own(mask)) * coef
    flow = (ocean_u + drag * (u - ocean_u), ocean_v + drag * (v - ocean_v))
    lane = lax.broadcasted_iota(jnp.int32, (rows, LANES), 1)
    strip = jnp.zeros((rows, LANES), jnp.float32)
    for k, f in enumerate((u, v, s1, s2, s12)):
        at = NSUB * k
        moved = pltpu.roll(f[:, cols:], at, 1) if at else f[:, cols:]
        strip = jnp.where((lane >= at) & (lane < at + NSUB), moved, strip)
    for k, f in enumerate(flow):
        velocity[k] = sea[...] * f[:, :cols]
        at = FLOW_LANE + NSUB * k
        strip = jnp.where((lane >= at) & (lane < at + NSUB), pltpu.roll(f[:, cols:], at, 1), strip)
    next_home = down[tall:, :]
    inland = lax.axis_index("gy") < picked.shape[0] - 1
    flagged = (lane >= HOME_LANE) & (lane < HOME_LANE + NSUB)
    for owner in range(pieces):
        flag = jnp.where(inland, jnp.where(next_home == float(owner), 1.0, 0.0), 0.0)
        picked[owner, 5] = jnp.where(flagged, flag, strip)
    here = [jnp.concatenate([chosen[k]] * (rows // 8), axis=0) > 0.5 for k in range(pieces * pieces)]
    for k, f in enumerate((u, v, s1, s2, s12)):
        blocks = [f[:, LANES * b : LANES * (b + 1)] for b in range(pieces)]
        for owner in range(pieces):
            value = jnp.zeros_like(blocks[0])
            for b in range(pieces):
                value = jnp.where(here[owner * pieces + b], blocks[b], value)
            picked[owner, k] = value


def tracer_kernel(
    warm, salt, sea_in, icy, cover, volume, up, down, inner, outer,
    warm_out, salt_out, coef, cut_low, cut_high, gain, rise,
):
    step = pl.program_id(0)
    levels, rows, cols = warm.shape
    count = warm_out.shape[0]
    low, high = up[...], down[rows + 2 * NSUB :, :]
    top = NICE * NSUB

    @pl.when(step == 0)
    def _():
        lane = lax.broadcasted_iota(jnp.int32, (rows, cols), 1)
        row = lax.broadcasted_iota(jnp.int32, (rows, cols), 0)
        short = lax.broadcasted_iota(jnp.int32, (rows, LANES), 1)
        sea = sea_in[...]
        mine = DIFFUSIVITY * sea
        east = jnp.where(row < rows - 1, mine * pltpu.roll(sea, rows - 1, 0), 0.0)
        west = jnp.where(row > 0, mine * pltpu.roll(sea, 1, 0), 0.0)
        north = jnp.where(lane < cols - 1, mine * pltpu.roll(sea, cols - 1, 1), 0.0)
        south = jnp.where(lane > 0, mine * pltpu.roll(sea, 1, 1), 0.0)
        at = 2 * levels
        edge_low = jnp.where(short == 0, mine[:, :LANES] * pltpu.roll(low, LANES - at, 1), 0.0)
        edge_high = jnp.where(
            short == LANES - 1,
            mine[:, cols - LANES :] * pltpu.roll(high, LANES - 1 - at, 1),
            0.0,
        )
        coef[1], coef[2], coef[3], coef[4] = east, west, north, south
        coef[0] = 1.0 - (east + west + north + south)
        coef[0, :, :LANES] -= edge_low
        coef[0, :, cols - LANES :] -= edge_high
        cut_low[...], cut_high[...] = edge_low, edge_high
        last, head = NSUB * WET_ROW + NSUB - 1, NSUB * WET_ROW

        def fluxes(from_east, from_west):
            east_gain = mine[rows - 1 :, :] * from_east[last : last + 1, :]
            west_gain = mine[:1, :] * from_west[head : head + 1, :]
            coef[0, rows - 1 :, :] -= east_gain
            coef[0, :1, :] -= west_gain
            rise[...] = east_gain * from_east[top:, :]
            gain[...] = west_gain * from_west[top:, :]

        @pl.when(even("grp"))
        def _():
            fluxes(inner, outer)

        @pl.when(jnp.logical_not(even("grp")))
        def _():
            fluxes(outer, inner)

    for part, (field, out) in enumerate(((warm, warm_out), (salt, salt_out))):
        for k in range(count):
            level = step * count + k
            f = field[level]
            out[k] = (
                coef[0] * f
                + coef[1] * pltpu.roll(f, rows - 1, 0)
                + coef[2] * pltpu.roll(f, 1, 0)
                + coef[3] * pltpu.roll(f, cols - 1, 1)
                + coef[4] * pltpu.roll(f, 1, 1)
            )
            plane = part * levels + level
            at = plane
            out[k, :, :LANES] += cut_low[...] * pltpu.roll(low, LANES - at, 1)
            out[k, :, cols - LANES :] += cut_high[...] * pltpu.roll(high, LANES - 1 - at, 1)
            out[k, rows - 1 :, :] += rise[pl.ds(plane, 1), :]
            out[k, :1, :] += gain[pl.ds(plane, 1), :]

    @pl.when(step == 0)
    def _():
        heat = jnp.zeros((rows, cols), jnp.float32)
        for k in range(cover.shape[0]):
            heat += HEAT_COEF * cover[k] * cover[k] / (volume[k] + THIN_LIMIT * cover[k])
        heat *= icy[...].astype(jnp.float32) * (warm[0] - FREEZING)
        warm_out[0] -= WARMTH_FACTOR * sea_in[...] * heat


def place_kernel(owned, velocity, sea, patch_out, velocity_out, patch, shifted, sems):
    tiles, _, rows, _ = owned.shape
    lane = lax.broadcasted_iota(jnp.int32, (rows, LANES), 1)
    for y in range(tiles):
        for k in range(5):
            value = owned[y, k]
            if y:
                strip = owned[y - 1, 5]
                sent = (lane < NSUB) & (pltpu.roll(strip, LANES - HOME_LANE, 1) > 0.5)
                moved = pltpu.roll(strip, LANES - NSUB * k, 1) if k else strip
                value = jnp.where(sent, moved, value)
            patch[k, :, LANES * y : LANES * (y + 1)] = value
    patch_copy = pltpu.make_async_copy(patch, patch_out, sems.at[0])
    patch_copy.start()
    at = lax.axis_index("gy")
    strip = owned[jnp.maximum(at - 1, 0), 5]
    for k in range(2):
        value = pltpu.roll(strip, LANES - FLOW_LANE - NSUB * k, 1)
        low = jnp.where(at > 0, lane, LANES) < NSUB
        shifted[k] = velocity[k]
        shifted[k, :, :LANES] = jnp.where(low, sea[:, :LANES] * value, velocity[k, :, :LANES])
    velocity_copy = pltpu.make_async_copy(shifted, velocity_out, sems.at[1])
    velocity_copy.start()
    patch_copy.wait()
    velocity_copy.wait()


def float_like(*shape):
    return jax.ShapeDtypeStruct(shape, jnp.float32)


def near(*shape):
    return pltpu.VMEM(shape, jnp.float32)


def held(*arrays):
    return tuple(pltpu.with_memory_space_constraint(a, pltpu.VMEM) for a in arrays)


def per_device(
    warm, salt, ocean, wind, ice, cover, volume, wet, icy, home
):
    levels, rows, cols = warm.shape
    grp, gy = lax.axis_size("grp"), lax.axis_size("gy")
    assert grp % 2 == 0 and gy % 2 == 0 and cols == gy * LANES
    swap = lambda pairs: [p for i, j in pairs for p in ((i, j), (j, i))]
    inner_pairs = swap([(i, i + 1) for i in range(0, grp, 2)])
    outer_pairs = swap([(i, (i + 1) % grp) for i in range(1, grp, 2)])
    up_pairs = [(i, i + 1) for i in range(gy - 1)]
    down_pairs = [(j, i) for i, j in up_pairs]
    tall = rows + 2 * NSUB
    tile = near(rows, LANES)
    message = near(NICE * NSUB + 2 * levels, cols)


    sources = (warm, salt, ocean, wind, ice, cover, volume, wet, icy)
    half = lambda a: a.shape[:-2] + (rows // 2, cols)
    anywhere = pl.BlockSpec(memory_space=pl.ANY)
    outer = pl.pallas_call(
        outer_kernel,
        out_shape=message,
        in_specs=[anywhere] * len(sources),
        out_specs=vmem(),
        scratch_shapes=[pltpu.VMEM(half(a), a.dtype) for a in sources[2:]]
        + [pltpu.SemaphoreType.DMA((len(sources) - 2,)), pltpu.SemaphoreType.DMA((2,))],
        name="outer_pack",
    )(*sources[2:], warm, salt)
    outer = lax.ppermute(outer, "grp", outer_pairs)
    blocks = home.shape[1]
    planes, inner, own, down, up, sea, chosen = pl.pallas_call(
        inner_kernel,
        out_shape=[
            near(NICE, rows, cols), message, tile, tile, tile, near(rows, cols), near(blocks * blocks, 8, LANES),
        ],
        in_specs=[vmem()] * 9 + [pl.BlockSpec(memory_space=pltpu.SMEM)],
        out_specs=[vmem()] * 7,
        name="inner_pack",
    )(*sources, home)
    inner = lax.ppermute(inner, "grp", inner_pairs)
    up = lax.ppermute(up, "gy", up_pairs)

    edge, down = pl.pallas_call(
        edge_kernel,
        out_shape=[near(NICE, 2 * NSUB, cols), near(tall + rows, LANES)],
        in_specs=[vmem()] * 4,
        out_specs=[vmem()] * 2,
        name="edge",
    )(*held(inner, outer, own, down))
    down = lax.ppermute(down, "gy", down_pairs)

    velocity, picked = pl.pallas_call(
        ice_kernel,
        out_shape=[near(2, rows, cols), float_like(gy, 6, rows, LANES)],
        in_specs=[vmem()] * 5,
        out_specs=[vmem()] * 2,
        name="ice",
    )(*held(planes, edge, down, sea, chosen))
    owned = lax.all_to_all(picked, "gy", split_axis=0, concat_axis=0, tiled=True)

    steps = 4
    block = pl.BlockSpec((levels // steps, rows, cols), lambda i: (i, 0, 0))
    warm_out, salt_out = pl.pallas_call(
        tracer_kernel,
        grid=(steps,),
        in_specs=[
            vmem(), vmem(), vmem(), spec(icy.shape), spec(cover.shape), spec(volume.shape),
            vmem(), vmem(), vmem(), vmem(),
        ],
        out_specs=[block, block],
        out_shape=[float_like(*warm.shape), float_like(*salt.shape)],
        scratch_shapes=[
            pltpu.VMEM((5, rows, cols), jnp.float32),
            pltpu.VMEM((rows, LANES), jnp.float32),
            pltpu.VMEM((rows, LANES), jnp.float32),
            pltpu.VMEM((2 * levels, cols), jnp.float32),
            pltpu.VMEM((2 * levels, cols), jnp.float32),
        ],
        name="tracers",
    )(warm, salt, *held(sea), icy, cover, volume, *held(up, down, inner, outer))

    patch, velocity = pl.pallas_call(
        place_kernel,
        out_shape=[float_like(5, rows, cols), float_like(2, rows, cols)],
        in_specs=[vmem()] * 3,
        out_specs=[anywhere] * 2,
        scratch_shapes=[
            pltpu.VMEM((5, rows, cols), jnp.float32),
            pltpu.VMEM((2, rows, cols), jnp.float32),
            pltpu.SemaphoreType.DMA((2,)),
        ],
        name="place",
    )(*held(owned, velocity, sea))
    return warm_out, salt_out, velocity, patch


def solution(mesh):
    field = P(None, "grp", "gy")
    flat = P("grp", "gy")

    return jax.shard_map(
        per_device,
        mesh=mesh,
        in_specs=(field,) * 7 + (flat,) * 3,
        out_specs=(field,) * 4,
        check_vma=False,
    )
```

```python
import jax
import jax.numpy as jnp
from jax import lax
from jax.experimental import pallas as pl
from jax.experimental.pallas import tpu as pltpu
from jax.sharding import PartitionSpec as P


NSUB = 4
DIFFUSIVITY = 0.2
STRENGTH_COEF = 20.0
MIN_MASS = 0.5
RELAX_RATE = 0.5
ECCENTRIC = 4.0
DELTA_FLOOR = 0.0025
SPEED_FLOOR = 0.01
CORIOLIS = 0.5
HEAT_COEF = 4.0
THIN_LIMIT = 0.1
FREEZING = -1.8
WARMTH_FACTOR = 0.05
STRESS_SCALE = 0.5

U, _, _, _, _, UO, VO, AREA, THICK, WX, WY, ICY = range(12)
NICE = 12
WET_ROW = WX
LANES = 128
REACH = 2 * NSUB
FLOW_LANE, HOME_LANE = 32, 64


def even(axis):
    return lax.rem(lax.axis_index(axis), 2) == 0


def spec(shape, index=None):
    zeros = (0,) * len(shape) if index is None else index
    return pl.BlockSpec(shape, lambda *_: zeros)


def vmem():
    return pl.BlockSpec(memory_space=pltpu.VMEM)


def outer_kernel(*refs):
    fields, warm, salt, out = refs[:7], refs[7], refs[8], refs[9]
    tiles, sems, row_sems = refs[10:17], refs[17], refs[18]
    levels, rows, _ = warm.shape
    half = rows // 2
    top = NICE * NSUB

    def message(start, row, wet_slot, edge_row):
        copies = [
            pltpu.make_async_copy(f.at[..., start : start + half, :], tile, sems.at[k])
            for k, (f, tile) in enumerate(zip(fields, tiles))
        ]
        lines = [
            pltpu.make_async_copy(
                f.at[:, start + edge_row, :], out.at[top + k * levels : top + (k + 1) * levels, :], row_sems.at[k]
            )
            for k, f in enumerate((warm, salt))
        ]
        for copy in copies + lines:
            copy.start()
        for copy in copies:
            copy.wait()
        ocean, wind, ice, cover, volume, wet, icy = tiles
        cut = slice(row, row + NSUB)
        planes = [ice[k, cut, :] for k in range(5)] + [ocean[0, cut, :], ocean[1, cut, :]]
        planes += [sum(f[k, cut, :] for k in range(f.shape[0])) for f in (cover, volume)]
        planes += [wind[0, cut, :], wind[1, cut, :], icy[cut, :].astype(jnp.float32)]
        for p in range(NICE):
            out[NSUB * p : NSUB * (p + 1), :] = planes[p]
        at = NSUB * WET_ROW + wet_slot
        out[at : at + 1, :] = wet[edge_row : edge_row + 1, :].astype(jnp.float32)
        for copy in lines:
            copy.wait()

    @pl.when(even("grp"))
    def _():
        message(0, 0, NSUB - 1, 0)

    @pl.when(jnp.logical_not(even("grp")))
    def _():
        message(half, half - NSUB, 0, half - 1)


def gathered(source, count):
    lane = lax.broadcasted_iota(jnp.int32, (count, LANES), 1)
    tile = jnp.zeros((count, LANES), jnp.float32)
    for p in range(NICE):
        here = (lane >= REACH * p) & (lane < REACH * (p + 1))
        tile = jnp.where(here, pltpu.roll(source[p, :, :LANES], REACH * p, 1), tile)
    return tile


def inner_kernel(*refs):
    warm, salt, fields = refs[0], refs[1], refs[2:9]
    planes, inner, sea = refs[9:12]
    tiles, sems, tile_sems = refs[12:19], refs[19], refs[20]
    ocean, wind, ice, cover, volume, wet, icy = tiles
    levels, rows, _ = warm.shape
    top = NICE * NSUB

    def message(row, wet_slot, edge_row):
        lines = [
            pltpu.make_async_copy(
                f.at[:, edge_row, :], inner.at[top + k * levels : top + (k + 1) * levels, :], sems.at[k]
            )
            for k, f in enumerate((warm, salt))
        ]
        copies = [
            pltpu.make_async_copy(f, held_tile, tile_sems.at[k])
            for k, (f, held_tile) in enumerate(zip(fields, tiles))
        ]
        for copy in copies + lines:
            copy.start()
        for copy in copies:
            copy.wait()
        for k in range(5):
            planes[U + k] = ice[k]
        planes[UO] = ocean[0]
        planes[VO] = ocean[1]
        planes[AREA] = sum(cover[k] for k in range(cover.shape[0]))
        planes[THICK] = sum(volume[k] for k in range(volume.shape[0]))
        planes[WX] = wind[0]
        planes[WY] = wind[1]
        planes[ICY] = icy[...].astype(jnp.float32)
        sea[...] = wet[...].astype(jnp.float32)
        for p in range(NICE):
            inner[NSUB * p : NSUB * (p + 1), :] = planes[p, row : row + NSUB, :]
        at = NSUB * WET_ROW + wet_slot
        inner[at : at + 1, :] = sea[edge_row : edge_row + 1, :]
        for copy in lines:
            copy.wait()

    @pl.when(even("grp"))
    def _():
        message(rows - NSUB, 0, rows - 1)

    @pl.when(jnp.logical_not(even("grp")))
    def _():
        message(0, NSUB - 1, 0)


def tiles_kernel(warm_low, warm_high, salt_low, salt_high, planes, sea, home, own, down, up, chosen):
    levels, rows, _ = warm_low.shape
    cols = sea.shape[1]
    blocks = home.shape[1]
    for owner in range(blocks):
        for b in range(blocks):
            flag = jnp.where(home[0, b] == owner, 1.0, 0.0)
            chosen[owner * blocks + b] = jnp.full(chosen.shape[1:], flag, jnp.float32)
    own[...] = gathered(planes, rows)
    lane = lax.broadcasted_iota(jnp.int32, (rows, LANES), 1)
    first_home = home[0, 0].astype(jnp.float32)
    low = jnp.where((lane >= HOME_LANE) & (lane < HOME_LANE + NSUB), first_home, 0.0)
    high = jnp.zeros((rows, LANES), jnp.float32)
    for p in range(2 * levels + 1):
        if p < levels:
            left, right = warm_low[p], warm_high[p]
        elif p < 2 * levels:
            left, right = salt_low[p - levels], salt_high[p - levels]
        else:
            left, right = sea[:, :LANES], sea[:, cols - LANES :]
        low = jnp.where(lane == p, pltpu.roll(left, p, 1), low)
        high = jnp.where(lane == p, pltpu.roll(right, p + 1, 1), high)
    down[...] = low
    up[...] = high


def edge_kernel(inner, outer, own, tracer, edge, down):
    rows = own.shape[0]

    def place(east, west):
        for p in range(NICE):
            edge[p, :NSUB, :] = east[NSUB * p : NSUB * (p + 1), :]
            edge[p, NSUB:, :] = west[NSUB * p : NSUB * (p + 1), :]

    @pl.when(even("grp"))
    def _():
        place(inner, outer)

    @pl.when(jnp.logical_not(even("grp")))
    def _():
        place(outer, inner)

    tall = rows + 2 * NSUB
    down[:rows, :] = own[...]
    down[rows:tall, :] = gathered(edge, 2 * NSUB)
    down[tall:, :] = tracer[...]


def columns_of(tile, p):
    lane = lax.broadcasted_iota(jnp.int32, tile.shape, 1)
    return jnp.where(lane < REACH, tile if p == 0 else pltpu.roll(tile, LANES - REACH * p, 1), 0.0)


def root(square):
    return square * lax.rsqrt(square)


def ice_kernel(planes, edge, down, sea, chosen, velocity, picked):
    rows, cols = sea.shape
    pieces = cols // LANES
    tall = rows + 2 * NSUB
    broad = cols + LANES
    tile = down[:tall, :]
    wide = [
        jnp.concatenate(
            [jnp.concatenate([planes[p], edge[p]], axis=0), columns_of(tile, p)], axis=1
        )
        for p in range(NICE)
    ]
    east = lambda f: pltpu.roll(f, tall - 1, 0)
    west = lambda f: pltpu.roll(f, 1, 0)
    north = lambda f: pltpu.roll(f, broad - 1, 1)
    south = lambda f: pltpu.roll(f, 1, 1)
    area, thick, mask = wide[AREA], wide[THICK], wide[ICY]
    strength = (thick * jnp.exp(-STRENGTH_COEF * (1.0 - area))) * RELAX_RATE
    mass = thick + MIN_MASS
    keep = mask * (1.0 / (1.0 + RELAX_RATE))
    ocean_u, ocean_v = wide[UO], wide[VO]
    u, v, s1, s2, s12 = (wide[k] for k in range(5))
    for _ in range(NSUB):
        du, dv = east(u) - u, north(v) - v
        div, ten = du + dv, du - dv
        shr = (north(u) - u) + (east(v) - v)
        visc = strength * lax.rsqrt(
            div * div + (ten * ten + shr * shr) * (1.0 / ECCENTRIC) + DELTA_FLOOR
        )
        quarter = visc * (1.0 / ECCENTRIC)
        s1 = keep * (s1 + (visc * div - strength))
        s2 = keep * (s2 + quarter * ten)
        s12 = keep * (s12 + quarter * shr)
        total, gap = s1 + s2, s1 - s2
        force_u = 0.5 * (total - west(total)) + (s12 - south(s12))
        force_v = 0.5 * (gap - south(gap)) + (s12 - west(s12))
        coef = area * root((ocean_u - u) ** 2 + (ocean_v - v) ** 2 + SPEED_FLOOR)
        scale = mask / (mass + coef)
        turn = CORIOLIS * mass
        u, v = (
            scale * (mass * u + force_u + wide[WX] + coef * ocean_u + turn * v),
            scale * (mass * v + force_v + wide[WY] + coef * ocean_v - turn * u),
        )
    own = lambda f: f[:rows, :]
    u, v, s1, s2, s12, ocean_u, ocean_v = (own(f) for f in (u, v, s1, s2, s12, ocean_u, ocean_v))
    coef = own(area) * root((ocean_u - u) ** 2 + (ocean_v - v) ** 2 + SPEED_FLOOR)
    drag = (STRESS_SCALE * own(mask)) * coef
    flow = (ocean_u + drag * (u - ocean_u), ocean_v + drag * (v - ocean_v))
    lane = lax.broadcasted_iota(jnp.int32, (rows, LANES), 1)
    strip = jnp.zeros((rows, LANES), jnp.float32)
    for k, f in enumerate((u, v, s1, s2, s12)):
        at = NSUB * k
        moved = pltpu.roll(f[:, cols:], at, 1) if at else f[:, cols:]
        strip = jnp.where((lane >= at) & (lane < at + NSUB), moved, strip)
    for k, f in enumerate(flow):
        velocity[k] = sea[...] * f[:, :cols]
        at = FLOW_LANE + NSUB * k
        strip = jnp.where((lane >= at) & (lane < at + NSUB), pltpu.roll(f[:, cols:], at, 1), strip)
    next_home = down[tall:, :]
    inland = lax.axis_index("gy") < picked.shape[0] - 1
    flagged = (lane >= HOME_LANE) & (lane < HOME_LANE + NSUB)
    for owner in range(pieces):
        flag = jnp.where(inland, jnp.where(next_home == float(owner), 1.0, 0.0), 0.0)
        picked[owner, 5] = jnp.where(flagged, flag, strip)
    here = [jnp.concatenate([chosen[k]] * (rows // 8), axis=0) > 0.5 for k in range(pieces * pieces)]
    for k, f in enumerate((u, v, s1, s2, s12)):
        blocks = [f[:, LANES * b : LANES * (b + 1)] for b in range(pieces)]
        for owner in range(pieces):
            value = jnp.zeros_like(blocks[0])
            for b in range(pieces):
                value = jnp.where(here[owner * pieces + b], blocks[b], value)
            picked[owner, k] = value


def tracer_kernel(
    warm, salt, sea_in, icy, cover, volume, up, down, inner, outer,
    warm_out, salt_out, coef, cut_low, cut_high, gain, rise,
):
    step = pl.program_id(0)
    levels, rows, cols = warm.shape
    count = warm_out.shape[0]
    low, high = up[...], down[rows + 2 * NSUB :, :]
    top = NICE * NSUB

    @pl.when(step == 0)
    def _():
        lane = lax.broadcasted_iota(jnp.int32, (rows, cols), 1)
        row = lax.broadcasted_iota(jnp.int32, (rows, cols), 0)
        short = lax.broadcasted_iota(jnp.int32, (rows, LANES), 1)
        sea = sea_in[...]
        mine = DIFFUSIVITY * sea
        east = jnp.where(row < rows - 1, mine * pltpu.roll(sea, rows - 1, 0), 0.0)
        west = jnp.where(row > 0, mine * pltpu.roll(sea, 1, 0), 0.0)
        north = jnp.where(lane < cols - 1, mine * pltpu.roll(sea, cols - 1, 1), 0.0)
        south = jnp.where(lane > 0, mine * pltpu.roll(sea, 1, 1), 0.0)
        at = 2 * levels
        edge_low = jnp.where(short == 0, mine[:, :LANES] * pltpu.roll(low, LANES - at, 1), 0.0)
        edge_high = jnp.where(
            short == LANES - 1,
            mine[:, cols - LANES :] * pltpu.roll(high, LANES - 1 - at, 1),
            0.0,
        )
        coef[1], coef[2], coef[3], coef[4] = east, west, north, south
        coef[0] = 1.0 - (east + west + north + south)
        coef[0, :, :LANES] -= edge_low
        coef[0, :, cols - LANES :] -= edge_high
        cut_low[...], cut_high[...] = edge_low, edge_high
        last, head = NSUB * WET_ROW + NSUB - 1, NSUB * WET_ROW

        def fluxes(from_east, from_west):
            east_gain = mine[rows - 1 :, :] * from_east[last : last + 1, :]
            west_gain = mine[:1, :] * from_west[head : head + 1, :]
            coef[0, rows - 1 :, :] -= east_gain
            coef[0, :1, :] -= west_gain
            rise[...] = east_gain * from_east[top:, :]
            gain[...] = west_gain * from_west[top:, :]

        @pl.when(even("grp"))
        def _():
            fluxes(inner, outer)

        @pl.when(jnp.logical_not(even("grp")))
        def _():
            fluxes(outer, inner)

    for part, (field, out) in enumerate(((warm, warm_out), (salt, salt_out))):
        for k in range(count):
            level = step * count + k
            f = field[level]
            out[k] = (
                coef[0] * f
                + coef[1] * pltpu.roll(f, rows - 1, 0)
                + coef[2] * pltpu.roll(f, 1, 0)
                + coef[3] * pltpu.roll(f, cols - 1, 1)
                + coef[4] * pltpu.roll(f, 1, 1)
            )
            plane = part * levels + level
            at = plane
            out[k, :, :LANES] += cut_low[...] * pltpu.roll(low, LANES - at, 1)
            out[k, :, cols - LANES :] += cut_high[...] * pltpu.roll(high, LANES - 1 - at, 1)
            out[k, rows - 1 :, :] += rise[pl.ds(plane, 1), :]
            out[k, :1, :] += gain[pl.ds(plane, 1), :]

    @pl.when(step == 0)
    def _():
        heat = jnp.zeros((rows, cols), jnp.float32)
        for k in range(cover.shape[0]):
            heat += HEAT_COEF * cover[k] * cover[k] / (volume[k] + THIN_LIMIT * cover[k])
        heat *= icy[...].astype(jnp.float32) * (warm[0] - FREEZING)
        warm_out[0] -= WARMTH_FACTOR * sea_in[...] * heat


def place_kernel(owned, velocity, sea, patch_out, velocity_out, patch, shifted, sems):
    tiles, _, rows, _ = owned.shape
    lane = lax.broadcasted_iota(jnp.int32, (rows, LANES), 1)
    for y in range(tiles):
        for k in range(5):
            value = owned[y, k]
            if y:
                strip = owned[y - 1, 5]
                sent = (lane < NSUB) & (pltpu.roll(strip, LANES - HOME_LANE, 1) > 0.5)
                moved = pltpu.roll(strip, LANES - NSUB * k, 1) if k else strip
                value = jnp.where(sent, moved, value)
            patch[k, :, LANES * y : LANES * (y + 1)] = value
    patch_copy = pltpu.make_async_copy(patch, patch_out, sems.at[0])
    patch_copy.start()
    at = lax.axis_index("gy")
    strip = owned[jnp.maximum(at - 1, 0), 5]
    for k in range(2):
        value = pltpu.roll(strip, LANES - FLOW_LANE - NSUB * k, 1)
        low = jnp.where(at > 0, lane, LANES) < NSUB
        shifted[k] = velocity[k]
        shifted[k, :, :LANES] = jnp.where(low, sea[:, :LANES] * value, velocity[k, :, :LANES])
    velocity_copy = pltpu.make_async_copy(shifted, velocity_out, sems.at[1])
    velocity_copy.start()
    patch_copy.wait()
    velocity_copy.wait()


def float_like(*shape):
    return jax.ShapeDtypeStruct(shape, jnp.float32)


def near(*shape):
    return pltpu.VMEM(shape, jnp.float32)


def held(*arrays):
    return tuple(pltpu.with_memory_space_constraint(a, pltpu.VMEM) for a in arrays)


def per_device(
    warm, salt, ocean, wind, ice, cover, volume, wet, icy, home
):
    levels, rows, cols = warm.shape
    grp, gy = lax.axis_size("grp"), lax.axis_size("gy")
    assert grp % 2 == 0 and gy % 2 == 0 and cols == gy * LANES
    swap = lambda pairs: [p for i, j in pairs for p in ((i, j), (j, i))]
    inner_pairs = swap([(i, i + 1) for i in range(0, grp, 2)])
    outer_pairs = swap([(i, (i + 1) % grp) for i in range(1, grp, 2)])
    up_pairs = [(i, i + 1) for i in range(gy - 1)]
    down_pairs = [(j, i) for i, j in up_pairs]
    tall = rows + 2 * NSUB
    tile = near(rows, LANES)
    message = near(NICE * NSUB + 2 * levels, cols)


    sources = (warm, salt, ocean, wind, ice, cover, volume, wet, icy)
    half = lambda a: a.shape[:-2] + (rows // 2, cols)
    anywhere = pl.BlockSpec(memory_space=pl.ANY)
    outer = pl.pallas_call(
        outer_kernel,
        out_shape=message,
        in_specs=[anywhere] * len(sources),
        out_specs=vmem(),
        scratch_shapes=[pltpu.VMEM(half(a), a.dtype) for a in sources[2:]]
        + [pltpu.SemaphoreType.DMA((len(sources) - 2,)), pltpu.SemaphoreType.DMA((2,))],
        name="outer_pack",
    )(*sources[2:], warm, salt)
    outer = lax.ppermute(outer, "grp", outer_pairs)
    blocks = home.shape[1]
    planes, inner, sea = pl.pallas_call(
        inner_kernel,
        out_shape=[near(NICE, rows, cols), message, near(rows, cols)],
        in_specs=[anywhere] * len(sources),
        out_specs=[vmem()] * 3,
        scratch_shapes=[pltpu.VMEM(a.shape, a.dtype) for a in sources[2:]]
        + [pltpu.SemaphoreType.DMA((2,)), pltpu.SemaphoreType.DMA((len(sources) - 2,))],
        name="inner_pack",
    )(*sources)
    inner = lax.ppermute(inner, "grp", inner_pairs)
    ends = [spec((levels, rows, LANES)), spec((levels, rows, LANES), (0, 0, cols // LANES - 1))]
    own, down, up, chosen = pl.pallas_call(
        tiles_kernel,
        grid=(1,),
        out_shape=[tile, tile, tile, near(blocks * blocks, 8, LANES)],
        in_specs=ends * 2 + [vmem()] * 2 + [pl.BlockSpec(memory_space=pltpu.SMEM)],
        out_specs=[vmem()] * 4,
        name="tiles",
    )(warm, warm, salt, salt, *held(planes, sea), home)

    edge, down = pl.pallas_call(
        edge_kernel,
        out_shape=[near(NICE, 2 * NSUB, cols), near(tall + rows, LANES)],
        in_specs=[vmem()] * 4,
        out_specs=[vmem()] * 2,
        name="edge",
    )(*held(inner, outer, own, down))
    down = lax.ppermute(down, "gy", down_pairs)
    up = lax.ppermute(up, "gy", up_pairs)

    velocity, picked = pl.pallas_call(
        ice_kernel,
        out_shape=[near(2, rows, cols), float_like(gy, 6, rows, LANES)],
        in_specs=[vmem()] * 5,
        out_specs=[vmem()] * 2,
        name="ice",
    )(*held(planes, edge, down, sea, chosen))
    owned = lax.all_to_all(picked, "gy", split_axis=0, concat_axis=0, tiled=True)

    steps = 4
    block = pl.BlockSpec((levels // steps, rows, cols), lambda i: (i, 0, 0))
    warm_out, salt_out = pl.pallas_call(
        tracer_kernel,
        grid=(steps,),
        in_specs=[
            vmem(), vmem(), vmem(), spec(icy.shape), spec(cover.shape), spec(volume.shape),
            vmem(), vmem(), vmem(), vmem(),
        ],
        out_specs=[block, block],
        out_shape=[float_like(*warm.shape), float_like(*salt.shape)],
        scratch_shapes=[
            pltpu.VMEM((5, rows, cols), jnp.float32),
            pltpu.VMEM((rows, LANES), jnp.float32),
            pltpu.VMEM((rows, LANES), jnp.float32),
            pltpu.VMEM((2 * levels, cols), jnp.float32),
            pltpu.VMEM((2 * levels, cols), jnp.float32),
        ],
        name="tracers",
    )(warm, salt, *held(sea), icy, cover, volume, *held(up, down, inner, outer))

    patch, velocity = pl.pallas_call(
        place_kernel,
        out_shape=[float_like(5, rows, cols), float_like(2, rows, cols)],
        in_specs=[vmem()] * 3,
        out_specs=[anywhere] * 2,
        scratch_shapes=[
            pltpu.VMEM((5, rows, cols), jnp.float32),
            pltpu.VMEM((2, rows, cols), jnp.float32),
            pltpu.SemaphoreType.DMA((2,)),
        ],
        name="place",
    )(*held(owned, velocity, sea))
    return warm_out, salt_out, velocity, patch


def solution(mesh):
    field = P(None, "grp", "gy")
    flat = P("grp", "gy")

    return jax.shard_map(
        per_device,
        mesh=mesh,
        in_specs=(field,) * 7 + (flat,) * 3,
        out_specs=(field,) * 4,
        check_vma=False,
    )
```
